32 devices in a mesh: blk: 8 (over z, x), col: 4 (over y, core).
Axes of the slice: x: 2, y: 2, z: 4, core: 2. Of those that a mesh axis runs over, the one named last changes fastest.
Arguments:
- points: bfloat16 [4096, 128], P(('blk', 'col')), may hold values from -4.5 to 4.5
- targets: float32 [4096, 32], P(('blk', 'col')), may hold values from -6 to 6
- pivots: int32 [2, 256], replicated, may hold values from 0 to 4095, as said below
Outputs:
- factor: bfloat16 [4096, 512], P(('blk', 'col'))
- solution: float32 [4096, 32], P(('blk', 'col'))
- residual: float32 [4096, 32], P(('blk', 'col'))
The draws below stay inside these ranges and needn't reach their ends.
Inputs may be any that keep to these rules, and one draw needn't show every extreme that they name: `pivots`: the 512 indices are distinct; 0 and 4095 are among them.
All inputs are finite; a program needn't handle non-finite values.
Results may differ from the reference program's by a relative error of at most 0.012.
Values may be sent and summed in bfloat16 or wider, within the bound.
A program may use at most 64 MiB of HBM per device.

```python
import jax
import jax.numpy as jnp
from jax import lax

FEATURES = 128
PIV_BLOCK = 256
RHS_COLS = 32
ITERS = 3
POINTS = 4096


def draw_points(key, part):
    row_key, value_key = jax.random.split(key, 2)
    values = jnp.clip(jax.random.normal(value_key, (POINTS, FEATURES), jnp.float32), -4.5, 4.5)
    scales = jnp.exp(jax.random.uniform(row_key, (POINTS,), jnp.float32, jnp.log(0.25), jnp.log(1.0)))
    result = values * scales[:, None]
    return jnp.clip(result, -4.5, 4.5).astype(jnp.bfloat16)


def draw_pivots(key, part):
    first_key, second_key = jax.random.split(jax.random.fold_in(key, 11))
    middle = jax.random.permutation(first_key, POINTS - 2)[:2 * PIV_BLOCK - 2].astype(jnp.int32) + 1
    ends = jnp.array([0, POINTS - 1], dtype=jnp.int32)
    chosen = jnp.concatenate([ends, middle])
    return jax.random.permutation(second_key, chosen).astype(jnp.int32).reshape(2, PIV_BLOCK)


def levels(key, extent, shards, low, largest):
    def one(axis_at, shards_of):
        heights = jax.random.uniform(jax.random.fold_in(jax.random.fold_in(key, 6), axis_at), (shards_of,), jnp.float32, low / len(shards), largest / len(shards))
        return jnp.repeat(jnp.exp(heights), extent[axis_at] // shards_of).reshape((-1,) + (1,) * (len(extent) - axis_at - 1))

    factor_of = one(*shards[0])
    for cut in shards[1:]:
        factor_of = factor_of * one(*cut)
    return factor_of


def noise(own_key, dims, width, bound, cuts=(), held_as=jnp.bfloat16):
    drawn = jax.random.normal(own_key, dims, jnp.float32) * width
    if len(cuts) > 0:
        drawn = levels(own_key, dims, cuts, -0.22, 0.18) * drawn
    return jnp.clip(drawn, min=-bound, max=bound).astype(held_as)


def setup_inputs(seed: int = 0) -> dict:
    keys = jax.random.split(jax.random.key(seed), 4)
    return {
        "points": draw_points(jax.random.fold_in(keys[3], 71), 0),
        "targets": noise(keys[1], (POINTS, RHS_COLS), 1.0, 6.0, ((0, 32),), jnp.float32),
        "pivots": draw_pivots(jax.random.fold_in(keys[3], 71), 0),
    }


noise_level = 0.5
jitter_level = 0.05
highest = lax.Precision.HIGHEST

def squared_norms(point_rows):
    wide_rows = point_rows.astype(jnp.float32)
    return jnp.sum(wide_rows * wide_rows, axis=1)

def kernel_block(left_rows, left_norms, right_rows, right_norms):
    inner = lax.dot_general(left_rows.astype(jnp.float32), right_rows.astype(jnp.float32), (((1,), (1,)), ((), ())), preferred_element_type=jnp.float32)
    distance = left_norms[:, None] + right_norms[None, :] - 2.0 * inner
    return jnp.exp(-2.0 * distance / FEATURES)

def lower_solve(lower_factor, right_rows):
    return jax.scipy.linalg.solve_triangular(lower_factor, right_rows.T, lower=True).T

def build_factor(point_rows, first_pick, second_pick):
    row_norms = squared_norms(point_rows)
    first_norms = squared_norms(first_pick)
    second_norms = squared_norms(second_pick)
    identity_piv = jnp.eye(first_pick.shape[0], dtype=jnp.float32)
    first_chol = jnp.linalg.cholesky(kernel_block(first_pick, first_norms, first_pick, first_norms) + jitter_level * identity_piv)
    first_coef = lower_solve(first_chol, kernel_block(point_rows, row_norms, first_pick, first_norms))
    shared_coef = lower_solve(first_chol, kernel_block(second_pick, second_norms, first_pick, first_norms))
    schur_block = kernel_block(second_pick, second_norms, second_pick, second_norms) + jitter_level * identity_piv - jnp.dot(shared_coef, shared_coef.T, precision=highest)
    second_chol = jnp.linalg.cholesky(schur_block)
    second_cross = kernel_block(point_rows, row_norms, second_pick, second_norms) - jnp.dot(first_coef, shared_coef.T, precision=highest)
    second_coef = lower_solve(second_chol, second_cross)
    return jnp.concatenate([first_coef, second_coef], axis=1)

def reference(points, targets, pivots):
    wide_factor = build_factor(points, points[pivots[0]], points[pivots[1]])
    factor = wide_factor.astype(jnp.bfloat16)
    gram = lax.dot_general(wide_factor, wide_factor, (((0,), (0,)), ((), ())), precision=highest)
    gram = gram + noise_level * jnp.eye(2 * PIV_BLOCK, dtype=jnp.float32)
    gram_chol = jnp.linalg.cholesky(gram)
    row_norms = squared_norms(points)

    def precondition(residual_now):
        projection = lax.dot_general(wide_factor, residual_now, (((0,), (0,)), ((), ())), precision=highest)
        coefficients = jax.scipy.linalg.cho_solve((gram_chol, True), projection)
        return (residual_now - jnp.dot(wide_factor, coefficients, precision=highest)) / noise_level
    block_rows = min(POINTS, 512)
    block_count = POINTS // block_rows

    def kernel_product(directions):

        def one_block(operands):
            weights = kernel_block(operands[0], operands[1], points, row_norms)
            return jnp.dot(weights, directions, precision=highest)
        stacked = lax.map(one_block, (points.reshape(block_count, block_rows, FEATURES), row_norms.reshape(block_count, block_rows)))
        return stacked.reshape(POINTS, RHS_COLS) + noise_level * directions
    solution = jnp.zeros_like(targets)
    residual = targets
    direction_now = precondition(residual)
    inner_now = jnp.sum(residual * direction_now, axis=0)
    for step_index in range(ITERS):
        image = kernel_product(direction_now)
        step_size = inner_now / jnp.sum(direction_now * image, axis=0)
        solution = solution + step_size * direction_now
        residual = residual - step_size * image
        if step_index + 1 < ITERS:
            scaled = precondition(residual)
            inner_next = jnp.sum(residual * scaled, axis=0)
            direction_now = scaled + inner_next / inner_now * direction_now
            inner_now = inner_next
    return (factor, solution, residual)
```

```python
import functools

import jax
import jax.numpy as jnp
from jax import lax
from jax.experimental import pallas as pl
from jax.experimental.pallas import tpu as pltpu
from jax.sharding import PartitionSpec as P

FEATURES = 128
ITERS = 3
LANES = 128


noise_level = 0.5
jitter_level = 0.05
highest = lax.Precision.HIGHEST
MESH = pl.DeviceIdType.MESH


def squared_norms(point_rows):
    wide_rows = point_rows.astype(jnp.float32)
    return jnp.sum(wide_rows * wide_rows, axis=1)


def kernel_block(left_rows, left_norms, right_rows, right_norms):
    inner = lax.dot_general(
        left_rows, right_rows, (((1,), (1,)), ((), ())), preferred_element_type=jnp.float32
    )
    distance = left_norms[:, None] + right_norms[None, :] - 2.0 * inner
    return jnp.exp(-2.0 * distance / FEATURES)


def lower_solve(lower_factor, right_rows):
    return jax.scipy.linalg.solve_triangular(lower_factor, right_rows.T, lower=True).T


def build_factor(point_rows, first_pick, second_pick):
    row_norms = squared_norms(point_rows)
    first_norms = squared_norms(first_pick)
    second_norms = squared_norms(second_pick)
    identity_piv = jnp.eye(first_pick.shape[0], dtype=jnp.float32)
    first_chol = jnp.linalg.cholesky(
        kernel_block(first_pick, first_norms, first_pick, first_norms) + jitter_level * identity_piv
    )
    both = jnp.concatenate([point_rows, second_pick], axis=0)
    both_norms = jnp.concatenate([row_norms, second_norms], axis=0)
    both_coef = lower_solve(first_chol, kernel_block(both, both_norms, first_pick, first_norms))
    row_count = point_rows.shape[0]
    first_coef, shared_coef = both_coef[:row_count], both_coef[row_count:]
    schur_block = (
        kernel_block(second_pick, second_norms, second_pick, second_norms)
        + jitter_level * identity_piv
        - jnp.dot(shared_coef, shared_coef.T, precision=highest)
    )
    second_chol = jnp.linalg.cholesky(schur_block)
    second_cross = kernel_block(point_rows, row_norms, second_pick, second_norms) - jnp.dot(
        first_coef, shared_coef.T, precision=highest
    )
    second_coef = lower_solve(second_chol, second_cross)
    return jnp.concatenate([first_coef, second_coef], axis=1)


def here(width):
    return lax.axis_index("blk") * width + lax.axis_index("col")


def coords(index, width):
    return (lax.div(index, width), lax.rem(index, width))


def greet(n, width, me):
    barrier = pltpu.get_barrier_semaphore()

    def hello(i, carry):
        peer = lax.rem(me + i, n)
        pl.semaphore_signal(
            barrier, inc=1, device_id=coords(peer, width), device_id_type=MESH
        )
        return carry

    lax.fori_loop(1, n, hello, 0)
    pl.semaphore_wait(barrier, n - 1)


def spread(n, width, me, src, dst, send_sem, recv_sem):
    def push(i, carry):
        peer = lax.rem(me + i, n)
        pltpu.make_async_remote_copy(
            src_ref=src(peer, i),
            dst_ref=dst(peer, i),
            send_sem=send_sem,
            recv_sem=recv_sem,
            device_id=coords(peer, width),
            device_id_type=MESH,
        ).start()
        return carry

    lax.fori_loop(1, n, push, 0)


def drain(ref, sem):
    pltpu.make_async_copy(ref, ref, sem).wait()


def gather_kernel(n, width, own_ref, all_ref, send_sem, recv_sem, own_sem):
    me = here(width)
    keep = pltpu.make_async_copy(own_ref, all_ref.at[me], own_sem)
    keep.start()
    greet(n, width, me)
    spread(
        n, width, me, lambda peer, i: own_ref, lambda peer, i: all_ref.at[me], send_sem, recv_sem
    )
    drain(all_ref.at[pl.ds(0, n - 1)], recv_sem)
    drain(all_ref.at[pl.ds(0, n - 1)], send_sem)
    keep.wait()


def gather_all(own, n, width):
    vmem = pl.BlockSpec(memory_space=pltpu.VMEM)
    return pl.pallas_call(
        functools.partial(gather_kernel, n, width),
        out_shape=jax.ShapeDtypeStruct((n,) + own.shape, own.dtype),
        in_specs=[vmem],
        out_specs=vmem,
        scratch_shapes=[pltpu.SemaphoreType.DMA] * 3,
        compiler_params=pltpu.CompilerParams(collective_id=0, has_side_effects=True),
        name="gather_points",
    )(own)


def reduce_kernel(n, width, part_ref, out_ref, got_ref, send_sem, recv_sem, send2_sem, recv2_sem):
    me = here(width)
    greet(n, width, me)
    spread(
        n,
        width,
        me,
        lambda peer, i: part_ref.at[peer],
        lambda peer, i: got_ref.at[i - 1],
        send_sem,
        recv_sem,
    )
    drain(got_ref, recv_sem)
    total = lax.fori_loop(0, n - 1, lambda i, acc: acc + got_ref[i], part_ref[me])
    out_ref[me] = total
    spread(
        n,
        width,
        me,
        lambda peer, i: out_ref.at[me],
        lambda peer, i: out_ref.at[me],
        send2_sem,
        recv2_sem,
    )
    drain(got_ref, send_sem)
    drain(got_ref, recv2_sem)
    drain(got_ref, send2_sem)


def reduce_all(part, n, width):
    vmem = pl.BlockSpec(memory_space=pltpu.VMEM)
    pieces = part.reshape(n, part.shape[0] // n, part.shape[1])
    summed = pl.pallas_call(
        functools.partial(reduce_kernel, n, width),
        out_shape=jax.ShapeDtypeStruct(pieces.shape, pieces.dtype),
        in_specs=[vmem],
        out_specs=vmem,
        scratch_shapes=[pltpu.VMEM((n - 1,) + pieces.shape[1:], pieces.dtype)]
        + [pltpu.SemaphoreType.DMA] * 4,
        compiler_params=pltpu.CompilerParams(collective_id=1, has_side_effects=True),
        name="sum_gram",
    )(pieces)
    return summed.reshape(part.shape)


def cg_kernel(
    n,
    width,
    owners,
    tile_ref,
    rhs_ref,
    wide_ref,
    inverse_ref,
    sol_ref,
    res_ref,
    dirs,
    put,
    got,
    ans,
    kept_proj,
    kept_squares,
    kept_rz,
    dir_send,
    dir_recv,
    put_send,
    put_recv,
    ans_send,
    ans_recv,
):
    me = here(width)
    rhs_count, row_count = rhs_ref.shape
    per = rhs_count // owners
    order = wide_ref.shape[1]
    lanes = order // LANES
    all_own = owners == n
    greet(n, width, me)

    def only_owners(body):
        if all_own:
            body()
        else:
            pl.when(me < owners)(body)

    def wide_sum(values):
        return jnp.broadcast_to(jnp.sum(values, axis=1, keepdims=True), (values.shape[0], LANES))

    def to_owners(k, proj, sums):
        for q in range(lanes):
            put[k, :, q, :] = proj[:, q * LANES : (q + 1) * LANES]
        for s, value in enumerate(sums):
            put[k, :, lanes + s, :] = value

        def push(i, carry):
            peer = lax.rem(me + i, owners)

            def go():
                pltpu.make_async_remote_copy(
                    src_ref=put.at[k, pl.ds(peer * per, per)],
                    dst_ref=got.at[k, lax.rem(me - peer + n, n) - 1],
                    send_sem=put_send.at[k],
                    recv_sem=put_recv.at[k],
                    device_id=coords(peer, width),
                    device_id_type=MESH,
                ).start()

            if all_own:
                go()
            else:
                pl.when(peer != me)(go)
            return carry

        lax.fori_loop(1 if all_own else 0, owners, push, 0)

    def finish_put(k):
        if all_own:
            drain(put.at[k, pl.ds(0, (owners - 1) * per)], put_send.at[k])
        else:

            @pl.when(me < owners)
            def _():
                drain(put.at[k, pl.ds(0, (owners - 1) * per)], put_send.at[k])

            @pl.when(me >= owners)
            def _():
                drain(put.at[k], put_send.at[k])

    def collect(k):
        drain(got.at[k], put_recv.at[k])
        start = put[k, pl.ds(me * per, per)]
        return lax.fori_loop(0, n - 1, lambda i, acc: acc + got[k, i], start)

    def answer(k, rows):
        for s, value in enumerate(rows):
            ans[k, pl.ds(me * per, per), s, :] = value
        spread(
            n,
            width,
            me,
            lambda peer, i: ans.at[k, pl.ds(me * per, per)],
            lambda peer, i: ans.at[k, pl.ds(me * per, per)],
            ans_send.at[k],
            ans_recv.at[k],
        )

    def await_answer(k):
        if all_own:
            drain(ans.at[k, pl.ds(0, (owners - 1) * per)], ans_recv.at[k])
        else:

            @pl.when(me < owners)
            def _():
                drain(ans.at[k, pl.ds(0, (owners - 1) * per)], ans_recv.at[k])

            @pl.when(me >= owners)
            def _():
                drain(ans.at[k], ans_recv.at[k])

    def finish_answer(k):
        def body():
            def one(i, carry):
                drain(ans.at[k, pl.ds(0, per)], ans_send.at[k])
                return carry

            lax.fori_loop(1, n, one, 0)

        only_owners(body)

    def solve(proj):
        half = lax.dot_general(
            proj,
            inverse_ref[...],
            (((1,), (1,)), ((), ())),
            precision=highest,
            preferred_element_type=jnp.float32,
        )
        coef = jnp.dot(
            half, inverse_ref[...], precision=highest, preferred_element_type=jnp.float32
        )
        return coef, wide_sum(half * half)

    def split(row):
        return [row[:, q * LANES : (q + 1) * LANES] for q in range(lanes)]

    def project(rows):
        return jnp.dot(rows, wide_ref[...], precision=highest, preferred_element_type=jnp.float32)

    def joined(packed):
        return jnp.concatenate([packed[:, q, :] for q in range(lanes)], axis=1)

    def precondition(residual, k):
        packed = ans[k]
        back = lax.dot_general(
            joined(packed),
            wide_ref[...],
            (((1,), (1,)), ((), ())),
            precision=highest,
            preferred_element_type=jnp.float32,
        )
        return (residual - back) * (1.0 / noise_level)

    residual = rhs_ref[...]
    solution = jnp.zeros_like(residual)
    to_owners(0, project(residual), [wide_sum(residual * residual)])

    def first_answer():
        total = collect(0)
        proj = joined(total)
        squares = total[:, lanes, :]
        coef, covered = solve(proj)
        kept_proj[...] = proj
        kept_squares[...] = squares
        kept_rz[...] = (squares - covered) * (1.0 / noise_level)
        answer(0, split(coef))

    def later_answer(k, last):
        total = collect(k)
        rz_before = kept_rz[...]
        size = rz_before / total[:, lanes, :]
        if last:
            answer(k, [size] * (lanes + 2))
            return
        along, image_squares = total[:, lanes + 1, :], total[:, lanes + 2, :]
        size_row = jnp.concatenate([size] * lanes, axis=1)
        proj = kept_proj[...] - size_row * joined(total)
        squares = kept_squares[...] - 2.0 * size * along + size * size * image_squares
        coef, covered = solve(proj)
        rz = (squares - covered) * (1.0 / noise_level)
        kept_proj[...] = proj
        kept_squares[...] = squares
        kept_rz[...] = rz
        answer(k, split(coef) + [size, rz / rz_before])

    only_owners(first_answer)
    await_answer(0)
    direction = precondition(residual, 0)

    for step_index in range(ITERS):
        last = step_index + 1 == ITERS
        dirs[step_index, me] = direction
        spread(
            n,
            width,
            me,
            lambda peer, i: dirs.at[step_index, me],
            lambda peer, i: dirs.at[step_index, me],
            dir_send.at[step_index],
            dir_recv.at[step_index],
        )
        drain(dirs.at[step_index, pl.ds(0, n - 1)], dir_recv.at[step_index])

        def multiply(j, acc):
            return acc + jnp.dot(
                dirs[step_index, j],
                tile_ref[j],
                precision=highest,
                preferred_element_type=jnp.float32,
            )

        image = lax.fori_loop(0, n, multiply, noise_level * direction, unroll=4)
        k = step_index + 1
        sums = [wide_sum(direction * image)]
        if last:
            to_owners(k, jnp.zeros((rhs_count, order), jnp.float32), sums)
        else:
            to_owners(
                k, project(image), sums + [wide_sum(residual * image), wide_sum(image * image)]
            )
        only_owners(functools.partial(later_answer, k, last))
        await_answer(k)
        size = ans[k, :, lanes, :]
        solution = solution + size * direction
        residual = residual - size * image
        if not last:
            direction = precondition(residual, k) + ans[k, :, lanes + 1, :] * direction
    sol_ref[...] = solution
    res_ref[...] = residual
    for step_index in range(ITERS):
        drain(dirs.at[step_index, pl.ds(0, n - 1)], dir_send.at[step_index])
    for k in range(ITERS + 1):
        finish_put(k)
        finish_answer(k)


def solve_cg(tile, targets_t, wide_factor, inverse, n, width):
    rhs_count, row_count = targets_t.shape
    owners = min(n, rhs_count)
    per = rhs_count // owners
    order = wide_factor.shape[1]
    rows = -(-(order // LANES + 3) // 8) * 8
    vmem = pl.BlockSpec(memory_space=pltpu.VMEM)
    f32 = jnp.float32
    return pl.pallas_call(
        functools.partial(cg_kernel, n, width, owners),
        out_shape=[jax.ShapeDtypeStruct((rhs_count, row_count), f32)] * 2,
        in_specs=[vmem] * 4,
        out_specs=[vmem] * 2,
        scratch_shapes=[
            pltpu.VMEM((ITERS, n, rhs_count, row_count), f32),
            pltpu.VMEM((ITERS + 1, rhs_count, rows, LANES), f32),
            pltpu.VMEM((ITERS + 1, n - 1, per, rows, LANES), f32),
            pltpu.VMEM((ITERS + 1, rhs_count, rows, LANES), f32),
            pltpu.VMEM((per, order), f32),
            pltpu.VMEM((per, LANES), f32),
            pltpu.VMEM((per, LANES), f32),
            pltpu.SemaphoreType.DMA((ITERS,)),
            pltpu.SemaphoreType.DMA((ITERS,)),
        ]
        + [pltpu.SemaphoreType.DMA((ITERS + 1,))] * 4,
        compiler_params=pltpu.CompilerParams(collective_id=2, has_side_effects=True),
        name="conjugate_gradients",
    )(tile.reshape(n, row_count, row_count), targets_t, wide_factor, inverse)


def per_device(n, width, points, targets, pivots):
    piv_count = pivots.shape[1]
    all_points = gather_all(points, n, width)
    all_points = all_points.reshape(-1, points.shape[1])
    picked = all_points[pivots.reshape(-1)]
    wide_factor = build_factor(points, picked[:piv_count], picked[piv_count:])
    factor = wide_factor.astype(jnp.bfloat16)
    local_gram = lax.dot_general(
        wide_factor, wide_factor, (((0,), (0,)), ((), ())), precision=highest
    )
    gram = reduce_all(local_gram, n, width)
    identity = jnp.eye(2 * piv_count, dtype=jnp.float32)
    gram_chol = jnp.linalg.cholesky(gram + noise_level * identity)
    inverse = jax.scipy.linalg.solve_triangular(gram_chol, identity, lower=True)
    tile = kernel_block(all_points, squared_norms(all_points), points, squared_norms(points))
    solution_t, residual_t = solve_cg(tile, targets.T, wide_factor, inverse, n, width)
    return (factor, solution_t.T, residual_t.T)


def solution(mesh):
    n, width = mesh.size, mesh.shape["col"]
    return jax.shard_map(
        functools.partial(per_device, n, width),
        mesh=mesh,
        in_specs=(P(("blk", "col"), None), P(("blk", "col"), None), P()),
        out_specs=(P(("blk", "col"), None), P(("blk", "col"), None), P(("blk", "col"), None)),
        check_vma=False,
    )
```

```python
import functools

import jax
import jax.numpy as jnp
from jax import lax
from jax.experimental import pallas as pl
from jax.experimental.pallas import tpu as pltpu
from jax.sharding import PartitionSpec as P

FEATURES = 128
ITERS = 3
LANES = 128


noise_level = 0.5
jitter_level = 0.05
highest = lax.Precision.HIGHEST
MESH = pl.DeviceIdType.MESH


def squared_norms(point_rows):
    wide_rows = point_rows.astype(jnp.float32)
    return jnp.sum(wide_rows * wide_rows, axis=1)


def kernel_block(left_rows, left_norms, right_rows, right_norms):
    inner = lax.dot_general(
        left_rows, right_rows, (((1,), (1,)), ((), ())), preferred_element_type=jnp.float32
    )
    distance = left_norms[:, None] + right_norms[None, :] - 2.0 * inner
    return jnp.exp(-2.0 * distance / FEATURES)


def chol_inverse(matrix):
    size = matrix.shape[0]
    if size <= LANES:
        lower = lax.linalg.cholesky(matrix, symmetrize_input=False)
        return jax.scipy.linalg.solve_triangular(
            lower, jnp.eye(size, dtype=jnp.float32), lower=True
        )
    half = size // 2
    top = chol_inverse(matrix[:half, :half])
    side = jnp.dot(matrix[half:, :half], top.T, precision=highest)
    low = chol_inverse(matrix[half:, half:] - jnp.dot(side, side.T, precision=highest))
    cross = -jnp.dot(low, jnp.dot(side, top, precision=highest), precision=highest)
    return jnp.concatenate(
        [
            jnp.concatenate([top, jnp.zeros_like(cross.T)], axis=1),
            jnp.concatenate([cross, low], axis=1),
        ],
        axis=0,
    )


def build_factor(point_rows, picked):
    picked_norms = squared_norms(picked)
    identity = jnp.eye(picked.shape[0], dtype=jnp.float32)
    inverse = chol_inverse(
        kernel_block(picked, picked_norms, picked, picked_norms) + jitter_level * identity
    )
    cross = kernel_block(point_rows, squared_norms(point_rows), picked, picked_norms)
    return jnp.dot(cross, inverse.T, precision=highest)


def lower_blocks(count):
    return [(i, j) for i in range(count) for j in range(i + 1)]


def pack_lower(matrix):
    count = matrix.shape[0] // LANES
    return jnp.concatenate(
        [
            matrix[i * LANES : (i + 1) * LANES, j * LANES : (j + 1) * LANES]
            for i, j in lower_blocks(count)
        ],
        axis=0,
    )


def unpack_lower(packed, order):
    count = order // LANES
    blocks = {
        at: packed[k * LANES : (k + 1) * LANES] for k, at in enumerate(lower_blocks(count))
    }
    empty = jnp.zeros((LANES, LANES), packed.dtype)
    return jnp.concatenate(
        [
            jnp.concatenate([blocks.get((i, j), empty) for j in range(count)], axis=1)
            for i in range(count)
        ],
        axis=0,
    )


def here(width):
    return lax.axis_index("blk") * width + lax.axis_index("col")


def coords(index, width):
    return (lax.div(index, width), lax.rem(index, width))


def greet(n, width, me):
    barrier = pltpu.get_barrier_semaphore()

    def hello(i, carry):
        peer = lax.rem(me + i, n)
        pl.semaphore_signal(
            barrier, inc=1, device_id=coords(peer, width), device_id_type=MESH
        )
        return carry

    lax.fori_loop(1, n, hello, 0)
    pl.semaphore_wait(barrier, n - 1)


def spread(n, width, me, src, dst, send_sem, recv_sem):
    def push(i, carry):
        peer = lax.rem(me + i, n)
        pltpu.make_async_remote_copy(
            src_ref=src(peer, i),
            dst_ref=dst(peer, i),
            send_sem=send_sem,
            recv_sem=recv_sem,
            device_id=coords(peer, width),
            device_id_type=MESH,
        ).start()
        return carry

    lax.fori_loop(1, n, push, 0)


def drain(ref, sem):
    pltpu.make_async_copy(ref, ref, sem).wait()


def gather_kernel(n, width, own_ref, all_ref, send_sem, recv_sem, own_sem):
    me = here(width)
    keep = pltpu.make_async_copy(own_ref, all_ref.at[me], own_sem)
    keep.start()
    greet(n, width, me)
    spread(
        n, width, me, lambda peer, i: own_ref, lambda peer, i: all_ref.at[me], send_sem, recv_sem
    )
    drain(all_ref.at[pl.ds(0, n - 1)], recv_sem)
    drain(all_ref.at[pl.ds(0, n - 1)], send_sem)
    keep.wait()


def gather_all(own, n, width):
    vmem = pl.BlockSpec(memory_space=pltpu.VMEM)
    return pl.pallas_call(
        functools.partial(gather_kernel, n, width),
        out_shape=jax.ShapeDtypeStruct((n,) + own.shape, own.dtype),
        in_specs=[vmem],
        out_specs=vmem,
        scratch_shapes=[pltpu.SemaphoreType.DMA] * 3,
        compiler_params=pltpu.CompilerParams(collective_id=0, has_side_effects=True),
        name="gather_points",
    )(own)


def reduce_kernel(n, width, part_ref, out_ref, got_ref, send_sem, recv_sem, send2_sem, recv2_sem):
    me = here(width)
    greet(n, width, me)
    spread(
        n,
        width,
        me,
        lambda peer, i: part_ref.at[peer],
        lambda peer, i: got_ref.at[i - 1],
        send_sem,
        recv_sem,
    )
    drain(got_ref, recv_sem)
    total = lax.fori_loop(0, n - 1, lambda i, acc: acc + got_ref[i], part_ref[me])
    out_ref[me] = total
    spread(
        n,
        width,
        me,
        lambda peer, i: out_ref.at[me],
        lambda peer, i: out_ref.at[me],
        send2_sem,
        recv2_sem,
    )
    drain(got_ref, send_sem)
    drain(got_ref, recv2_sem)
    drain(got_ref, send2_sem)


def reduce_all(part, n, width):
    vmem = pl.BlockSpec(memory_space=pltpu.VMEM)
    pieces = part.reshape(n, part.shape[0] // n, part.shape[1])
    summed = pl.pallas_call(
        functools.partial(reduce_kernel, n, width),
        out_shape=jax.ShapeDtypeStruct(pieces.shape, pieces.dtype),
        in_specs=[vmem],
        out_specs=vmem,
        scratch_shapes=[pltpu.VMEM((n - 1,) + pieces.shape[1:], pieces.dtype)]
        + [pltpu.SemaphoreType.DMA] * 4,
        compiler_params=pltpu.CompilerParams(collective_id=1, has_side_effects=True),
        name="sum_gram",
    )(pieces)
    return summed.reshape(part.shape)


def cg_kernel(
    n,
    width,
    owners,
    tile_ref,
    rhs_ref,
    wide_ref,
    inverse_ref,
    sol_ref,
    res_ref,
    dirs,
    put,
    got,
    ans,
    kept_proj,
    kept_squares,
    kept_rz,
    dir_send,
    dir_recv,
    put_send,
    put_recv,
    ans_send,
    ans_recv,
):
    me = here(width)
    rhs_count, row_count = rhs_ref.shape
    per = rhs_count // owners
    order = wide_ref.shape[1]
    lanes = order // LANES
    all_own = owners == n
    greet(n, width, me)

    def only_owners(body):
        if all_own:
            body()
        else:
            pl.when(me < owners)(body)

    def wide_sum(values):
        return jnp.broadcast_to(jnp.sum(values, axis=1, keepdims=True), (values.shape[0], LANES))

    def to_owners(k, proj, sums):
        for q in range(lanes):
            put[k, :, q, :] = proj[:, q * LANES : (q + 1) * LANES]
        for s, value in enumerate(sums):
            put[k, :, lanes + s, :] = value

        def push(i, carry):
            peer = lax.rem(me + i, owners)

            def go():
                pltpu.make_async_remote_copy(
                    src_ref=put.at[k, pl.ds(peer * per, per)],
                    dst_ref=got.at[k, lax.rem(me - peer + n, n) - 1],
                    send_sem=put_send.at[k],
                    recv_sem=put_recv.at[k],
                    device_id=coords(peer, width),
                    device_id_type=MESH,
                ).start()

            if all_own:
                go()
            else:
                pl.when(peer != me)(go)
            return carry

        lax.fori_loop(1 if all_own else 0, owners, push, 0)

    def finish_put(k):
        if all_own:
            drain(put.at[k, pl.ds(0, (owners - 1) * per)], put_send.at[k])
        else:

            @pl.when(me < owners)
            def _():
                drain(put.at[k, pl.ds(0, (owners - 1) * per)], put_send.at[k])

            @pl.when(me >= owners)
            def _():
                drain(put.at[k], put_send.at[k])

    def collect(k):
        drain(got.at[k], put_recv.at[k])
        start = put[k, pl.ds(me * per, per)]
        return lax.fori_loop(0, n - 1, lambda i, acc: acc + got[k, i], start)

    def answer(k, rows):
        for s, value in enumerate(rows):
            ans[k, pl.ds(me * per, per), s, :] = value
        spread(
            n,
            width,
            me,
            lambda peer, i: ans.at[k, pl.ds(me * per, per)],
            lambda peer, i: ans.at[k, pl.ds(me * per, per)],
            ans_send.at[k],
            ans_recv.at[k],
        )

    def await_answer(k):
        if all_own:
            drain(ans.at[k, pl.ds(0, (owners - 1) * per)], ans_recv.at[k])
        else:

            @pl.when(me < owners)
            def _():
                drain(ans.at[k, pl.ds(0, (owners - 1) * per)], ans_recv.at[k])

            @pl.when(me >= owners)
            def _():
                drain(ans.at[k], ans_recv.at[k])

    def finish_answer(k):
        def body():
            def one(i, carry):
                drain(ans.at[k, pl.ds(0, per)], ans_send.at[k])
                return carry

            lax.fori_loop(1, n, one, 0)

        only_owners(body)

    def solve(proj):
        half = lax.dot_general(
            proj,
            inverse_ref[...],
            (((1,), (1,)), ((), ())),
            precision=highest,
            preferred_element_type=jnp.float32,
        )
        coef = jnp.dot(
            half, inverse_ref[...], precision=highest, preferred_element_type=jnp.float32
        )
        return coef, wide_sum(half * half)

    def split(row):
        return [row[:, q * LANES : (q + 1) * LANES] for q in range(lanes)]

    def project(rows):
        return jnp.dot(rows, wide_ref[...], precision=highest, preferred_element_type=jnp.float32)

    def joined(packed):
        return jnp.concatenate([packed[:, q, :] for q in range(lanes)], axis=1)

    def precondition(residual, k):
        packed = ans[k]
        back = lax.dot_general(
            joined(packed),
            wide_ref[...],
            (((1,), (1,)), ((), ())),
            precision=highest,
            preferred_element_type=jnp.float32,
        )
        return (residual - back) * (1.0 / noise_level)

    residual = rhs_ref[...]
    solution = jnp.zeros_like(residual)
    to_owners(0, project(residual), [wide_sum(residual * residual)])

    def first_answer():
        total = collect(0)
        proj = joined(total)
        squares = total[:, lanes, :]
        coef, covered = solve(proj)
        kept_proj[...] = proj
        kept_squares[...] = squares
        kept_rz[...] = (squares - covered) * (1.0 / noise_level)
        answer(0, split(coef))

    def later_answer(k, last):
        total = collect(k)
        rz_before = kept_rz[...]
        size = rz_before / total[:, lanes, :]
        if last:
            answer(k, [size] * (lanes + 2))
            return
        along, image_squares = total[:, lanes + 1, :], total[:, lanes + 2, :]
        size_row = jnp.concatenate([size] * lanes, axis=1)
        proj = kept_proj[...] - size_row * joined(total)
        squares = kept_squares[...] - 2.0 * size * along + size * size * image_squares
        coef, covered = solve(proj)
        rz = (squares - covered) * (1.0 / noise_level)
        kept_proj[...] = proj
        kept_squares[...] = squares
        kept_rz[...] = rz
        answer(k, split(coef) + [size, rz / rz_before])

    only_owners(first_answer)
    await_answer(0)
    direction = precondition(residual, 0)

    for step_index in range(ITERS):
        last = step_index + 1 == ITERS
        dirs[step_index, me] = direction
        spread(
            n,
            width,
            me,
            lambda peer, i: dirs.at[step_index, me],
            lambda peer, i: dirs.at[step_index, me],
            dir_send.at[step_index],
            dir_recv.at[step_index],
        )
        drain(dirs.at[step_index, pl.ds(0, n - 1)], dir_recv.at[step_index])

        def multiply(j, acc):
            return acc + jnp.dot(
                dirs[step_index, j],
                tile_ref[j],
                precision=highest,
                preferred_element_type=jnp.float32,
            )

        image = lax.fori_loop(0, n, multiply, noise_level * direction, unroll=4)
        k = step_index + 1
        sums = [wide_sum(direction * image)]
        if last:
            to_owners(k, jnp.zeros((rhs_count, order), jnp.float32), sums)
        else:
            to_owners(
                k, project(image), sums + [wide_sum(residual * image), wide_sum(image * image)]
            )
        only_owners(functools.partial(later_answer, k, last))
        await_answer(k)
        size = ans[k, :, lanes, :]
        solution = solution + size * direction
        residual = residual - size * image
        if not last:
            direction = precondition(residual, k) + ans[k, :, lanes + 1, :] * direction
    sol_ref[...] = solution
    res_ref[...] = residual
    for step_index in range(ITERS):
        drain(dirs.at[step_index, pl.ds(0, n - 1)], dir_send.at[step_index])
    for k in range(ITERS + 1):
        finish_put(k)
        finish_answer(k)


def solve_cg(tile, targets_t, wide_factor, inverse, n, width):
    rhs_count, row_count = targets_t.shape
    owners = min(n, rhs_count)
    per = rhs_count // owners
    order = wide_factor.shape[1]
    rows = -(-(order // LANES + 3) // 8) * 8
    vmem = pl.BlockSpec(memory_space=pltpu.VMEM)
    f32 = jnp.float32
    return pl.pallas_call(
        functools.partial(cg_kernel, n, width, owners),
        out_shape=[jax.ShapeDtypeStruct((rhs_count, row_count), f32)] * 2,
        in_specs=[vmem] * 4,
        out_specs=[vmem] * 2,
        scratch_shapes=[
            pltpu.VMEM((ITERS, n, rhs_count, row_count), f32),
            pltpu.VMEM((ITERS + 1, rhs_count, rows, LANES), f32),
            pltpu.VMEM((ITERS + 1, n - 1, per, rows, LANES), f32),
            pltpu.VMEM((ITERS + 1, rhs_count, rows, LANES), f32),
            pltpu.VMEM((per, order), f32),
            pltpu.VMEM((per, LANES), f32),
            pltpu.VMEM((per, LANES), f32),
            pltpu.SemaphoreType.DMA((ITERS,)),
            pltpu.SemaphoreType.DMA((ITERS,)),
        ]
        + [pltpu.SemaphoreType.DMA((ITERS + 1,))] * 4,
        compiler_params=pltpu.CompilerParams(collective_id=2, has_side_effects=True),
        name="conjugate_gradients",
    )(tile.reshape(n, row_count, row_count), targets_t, wide_factor, inverse)


def per_device(n, width, points, targets, pivots):
    piv_count = pivots.shape[1]
    all_points = gather_all(points, n, width)
    all_points = all_points.reshape(-1, points.shape[1])
    picked = all_points[pivots.reshape(-1)]
    wide_factor = build_factor(points, picked)
    factor = wide_factor.astype(jnp.bfloat16)
    local_gram = lax.dot_general(
        wide_factor, wide_factor, (((0,), (0,)), ((), ())), precision=highest
    )
    order = 2 * piv_count
    gram = unpack_lower(reduce_all(pack_lower(local_gram), n, width), order)
    inverse = chol_inverse(gram + noise_level * jnp.eye(order, dtype=jnp.float32))
    tile = kernel_block(all_points, squared_norms(all_points), points, squared_norms(points))
    solution_t, residual_t = solve_cg(tile, targets.T, wide_factor, inverse, n, width)
    return (factor, solution_t.T, residual_t.T)


def solution(mesh):
    n, width = mesh.size, mesh.shape["col"]
    return jax.shard_map(
        functools.partial(per_device, n, width),
        mesh=mesh,
        in_specs=(P(("blk", "col"), None), P(("blk", "col"), None), P()),
        out_specs=(P(("blk", "col"), None), P(("blk", "col"), None), P(("blk", "col"), None)),
        check_vma=False,
    )
```
